32 devices in a mesh: orb: 8 (over z, x), cell: 4 (over y, core).
Axes of the slice: x: 2, y: 2, z: 4, core: 2. Of those that a mesh axis runs over, the one named last changes fastest.
Arguments:
- potentials: bfloat16 [96, 65536], P(None, 'cell'), may hold values from -6 to 6
- orbitals: bfloat16 [512, 65536], P('orb', 'cell'), may hold values from -6 to 6
- levels: float32 [512], replicated, may hold values from 0.2 to 4
- occ_index: int32 [64], replicated, may hold values from 0 to 511, as said below
- coul_rows: float32 [256, 256], replicated, may hold values from -0.375 to 0.375
- coul_cols: float32 [256, 256], replicated, may hold values from -0.375 to 0.375
Outputs:
- screened: float32 [96, 256, 256], P('orb', 'cell')
The draws below stay inside these ranges and needn't reach their ends.
Inputs may be any that keep to these rules, and one draw needn't show every extreme that they name: `occ_index`: 64 distinct orbital numbers.
All inputs are finite; a program needn't handle non-finite values.
Results may differ from the reference program's by a relative error of at most 0.004.
Values may be sent and summed in bfloat16 or wider, within the bound.
A program may use at most 128 MiB of HBM per device.

```python
import math
import jax
import jax.numpy as jnp
from jax import lax

SIDE = 256
NORB = 512
NOCC = 64
NV = 96
POINTS = 65536


def draw_occ_index(key, part):
    return jax.random.permutation(jax.random.fold_in(key, 7), NORB)[:NOCC].astype(jnp.int32)


def block_levels(rng, extent, shards, low, largest):
    factor_of = 1.0
    for position, blocks in shards:
        heights = jax.random.uniform(jax.random.fold_in(jax.random.fold_in(rng, 6), position), (blocks,), jnp.float32, low / len(shards), largest / len(shards))
        factor_of = factor_of * jnp.repeat(jnp.exp(heights), extent[position] // blocks).reshape((-1,) + (1,) * (len(extent) - 1 - position))
    return factor_of


def centred(stream_key, shape, spread, bound, shards=(), kind=jnp.bfloat16):
    array = jax.random.normal(stream_key, shape, jnp.float32) * spread
    if len(shards) > 0:
        array = block_levels(stream_key, shape, shards, -0.22, 0.18) * array
    return jnp.clip(array, min=-bound, max=bound).astype(kind)


def setup_inputs(seed: int = 0) -> dict:
    arg_keys = jax.random.split(jax.random.key(seed), 7)
    potentials = centred(arg_keys[0], (NV, POINTS), 1.0, 6.0, ((1, 4),))
    orbitals = centred(arg_keys[1], (NORB, POINTS), 1.0, 6.0, ((0, 8), (1, 4)))
    levels = jnp.clip(jnp.exp(jax.random.uniform(arg_keys[2], (NORB,), jnp.float32, math.log(0.2), math.log(4.0))), 0.2, 4.0)
    occ_index = draw_occ_index(jax.random.fold_in(arg_keys[6], 71), 0)
    coul_rows = centred(arg_keys[4], (SIDE, SIDE), SIDE ** -0.5, 0.375, (), jnp.float32)
    coul_cols = centred(arg_keys[5], (SIDE, SIDE), SIDE ** -0.5, 0.375, (), jnp.float32)
    return dict(potentials=potentials, orbitals=orbitals, levels=levels, occ_index=occ_index, coul_rows=coul_rows, coul_cols=coul_cols)


def reference(potentials, orbitals, levels, occ_index, coul_rows, coul_cols):
    labels = jnp.arange(NORB, dtype=jnp.int32)
    marked = jnp.any(occ_index[:, None] == labels[None, :], axis=0)
    empty_mask = 1.0 - marked.astype(jnp.float32)
    volume = SIDE * SIDE
    basis = orbitals.astype(jnp.float32)

    def step(running, orbital_id):
        occ_row = lax.dynamic_index_in_dim(basis, orbital_id, 0, keepdims=False)
        products = (occ_row[None, :] * basis).astype(jnp.bfloat16)
        intersection = lax.dot_general(products, potentials, (((1,), (1,)), ((), ())), preferred_element_type=jnp.float32)
        occ_level = lax.dynamic_index_in_dim(levels, orbital_id, 0, keepdims=False)
        weights = -2.0 * empty_mask / (occ_level + levels)
        guess_block = (intersection * (weights / volume)[:, None]).astype(jnp.bfloat16)
        running = running + lax.dot_general(guess_block, products, (((0,), (0,)), ((), ())), preferred_element_type=jnp.float32)
        return running, None

    response, _ = lax.scan(step, jnp.zeros((NV, volume), jnp.float32), occ_index)
    plane = response.reshape(NV, SIDE, SIDE)
    by_columns = jnp.einsum("vrc,dc->vrd", plane, coul_cols, precision=lax.Precision.HIGHEST)
    screened = jnp.einsum("ab,vbc->vac", coul_rows, by_columns, precision=lax.Precision.HIGHEST)
    return screened
```

```python
import functools

import jax
import jax.numpy as jnp
import numpy as np
from jax import lax
from jax.experimental import pallas as pl
from jax.experimental.pallas import tpu as pltpu
from jax.sharding import PartitionSpec as P

SIDE = 256
GATHER_CHUNKS = 2
RESPONSE_CHUNKS = 4
VMEM = 56 * 1024 * 1024


def swap(x, axis, bit):
    n = lax.axis_size(axis)
    return lax.ppermute(x, axis, [(s, s ^ bit) for s in range(n)])


def upper(axis, bit):
    return (lax.axis_index(axis) // bit) % 2


def halve(x, axis, bit, dim, wire=None):
    half = x.shape[dim] // 2
    side = upper(axis, bit)
    keep = lax.dynamic_slice_in_dim(x, side * half, half, dim)
    send = lax.dynamic_slice_in_dim(x, (1 - side) * half, half, dim)
    if wire is not None:
        send = send.astype(wire)
    return keep + swap(send, axis, bit).astype(x.dtype)


def double(x, axis, bit, dim):
    other = swap(x, axis, bit)
    low = upper(axis, bit) == 0
    return jnp.concatenate([jnp.where(low, x, other), jnp.where(low, other, x)], dim)


def bits_of(axis):
    n = lax.axis_size(axis)
    return [1 << k for k in range(n.bit_length() - 1)]


def pair_rows(occ_ref, orb, first, count):
    return jnp.concatenate([occ_ref[i : i + 1, :] * orb for i in range(first, first + count)], 0)


def project_kernel(group, occ_ref, orb_ref, pot_ref, out_ref, acc):
    step = pl.program_id(0)

    @pl.when(step == 0)
    def _():
        acc[...] = jnp.zeros_like(acc)

    turned = pot_ref[...].T
    orb = orb_ref[...]
    rows = group * orb.shape[0]
    for k in range(occ_ref.shape[0] // group):
        pairs = pair_rows(occ_ref, orb, k * group, group)
        acc[k * rows : (k + 1) * rows, :] += jnp.dot(
            pairs, turned, preferred_element_type=jnp.float32
        )

    @pl.when(step == pl.num_programs(0) - 1)
    def _():
        out_ref[...] = acc[...].T


def project(occ, orbitals, potentials, start):
    slots, width = occ.shape
    stored = orbitals.shape[0]
    nv = potentials.shape[0]
    block = min(1024, width)
    shift = start // block
    pairs = slots * stored
    return pl.pallas_call(
        functools.partial(project_kernel, max(1, 256 // stored)),
        out_shape=jax.ShapeDtypeStruct((nv, pairs), jnp.float32),
        grid=(width // block,),
        in_specs=[
            pl.BlockSpec((slots, block), lambda s: (0, s)),
            pl.BlockSpec((stored, block), lambda s: (0, s + shift)),
            pl.BlockSpec((nv, block), lambda s: (0, s + shift)),
        ],
        out_specs=pl.BlockSpec((nv, pairs), lambda s: (0, 0)),
        scratch_shapes=[pltpu.VMEM((pairs, nv), jnp.float32)],
        compiler_params=pltpu.CompilerParams(vmem_limit_bytes=VMEM),
        cost_estimate=pl.CostEstimate(
            flops=2 * pairs * nv * width * 3,
            bytes_accessed=2 * width * (slots + stored + nv),
            transcendentals=0,
        ),
        name="project",
    )(occ, orbitals, potentials)


def respond_kernel(group, guess_ref, occ_ref, orb_ref, out_ref):
    orb = orb_ref[...]
    rows = group * orb.shape[0]
    total = None
    for k in range(occ_ref.shape[0] // group):
        pairs = pair_rows(occ_ref, orb, k * group, group)
        term = jnp.dot(
            guess_ref[:, k * rows : (k + 1) * rows], pairs, preferred_element_type=jnp.float32
        )
        total = term if total is None else total + term
    out_ref[...] = total


def respond(guess, occ, orbitals, start, occ_start, width):
    slots = occ.shape[0]
    stored = orbitals.shape[0]
    nv, pairs = guess.shape
    block = min(512, width)
    shift = start // block
    occ_shift = occ_start // block
    return pl.pallas_call(
        functools.partial(respond_kernel, max(1, 256 // stored)),
        out_shape=jax.ShapeDtypeStruct((nv, width), jnp.float32),
        grid=(width // block,),
        in_specs=[
            pl.BlockSpec((nv, pairs), lambda s: (0, 0)),
            pl.BlockSpec((slots, block), lambda s: (0, s + occ_shift)),
            pl.BlockSpec((stored, block), lambda s: (0, s + shift)),
        ],
        out_specs=pl.BlockSpec((nv, block), lambda s: (0, s)),
        compiler_params=pltpu.CompilerParams(vmem_limit_bytes=VMEM),
        cost_estimate=pl.CostEstimate(
            flops=2 * pairs * nv * width * 3,
            bytes_accessed=2 * width * (slots + stored) + 4 * nv * width,
            transcendentals=0,
        ),
        name="respond",
    )(guess, occ, orbitals)


def owner_order(nv, count, order):
    per = nv // count
    owners = []
    for place in range(count):
        owner = 0
        for depth, bit in enumerate(order):
            if (place >> (len(order) - 1 - depth)) & 1:
                owner |= bit
        owners.append(owner)
    return np.concatenate([np.arange(per) + o * per for o in owners])


def body(potentials, orbitals, levels, occ_index, coul_rows, coul_cols):
    nv, points_dev = potentials.shape
    volume = points_dev * lax.axis_size("cell")
    orb_count = lax.axis_size("orb")
    my_rank = lax.axis_index("orb")
    per_orb = orbitals.shape[0]
    slots = occ_index.shape[0]
    orb_bits = bits_of("orb")
    cell_bits = bits_of("cell")
    orders = [orb_bits, orb_bits[1:] + orb_bits[:1]]

    labels = jnp.arange(levels.shape[0], dtype=jnp.int32)
    marked = jnp.any(occ_index[:, None] == labels[None, :], axis=0)
    empty_all = 1.0 - marked.astype(jnp.float32)
    occ_hot = (occ_index[:, None] == labels[None, :]).astype(jnp.float32)
    occ_level = jnp.sum(occ_hot * levels[None, :], axis=1)
    basis_level = lax.dynamic_slice_in_dim(levels, my_rank * per_orb, per_orb)
    basis_empty = lax.dynamic_slice_in_dim(empty_all, my_rank * per_orb, per_orb)
    weights = -2.0 * basis_empty[None, :] / (occ_level[:, None] + basis_level[None, :])
    weights = (weights / volume).reshape(1, -1)

    owned_ids = my_rank * per_orb + jnp.arange(per_orb, dtype=jnp.int32)
    picker = (occ_index[:, None] == owned_ids[None, :]).astype(jnp.bfloat16)

    chunk = points_dev // GATHER_CHUNKS
    occ_parts = []
    for g in range(GATHER_CHUNKS):
        piece = jnp.dot(
            picker,
            orbitals[:, g * chunk : (g + 1) * chunk],
            preferred_element_type=jnp.float32,
        ).astype(jnp.bfloat16)
        order = orders[g % 2]
        for bit in order:
            piece = halve(piece, "orb", bit, 1)
        for bit in order[::-1]:
            piece = double(piece, "orb", bit, 1)
        occ_parts.append(piece)

    inter = None
    for g in range(GATHER_CHUNKS):
        part = project(occ_parts[g], orbitals, potentials, g * chunk)
        inter = part if inter is None else inter + part
    scale = weights
    for bit in cell_bits:
        inter = halve(inter, "cell", bit, 1)
        half = scale.shape[1] // 2
        scale = lax.dynamic_slice_in_dim(scale, upper("cell", bit) * half, half, 1)
    guess = (inter * scale).astype(jnp.bfloat16)
    for bit in cell_bits[::-1]:
        guess = double(guess, "cell", bit, 1)

    width = points_dev // RESPONSE_CHUNKS
    guesses = []
    for order in orders:
        rows = owner_order(nv, orb_count, order)
        place = jnp.asarray(rows[:, None] == np.arange(nv)[None, :], jnp.bfloat16)
        guesses.append(
            jnp.dot(place, guess, preferred_element_type=jnp.float32).astype(jnp.bfloat16)
        )
    owned = []
    for r in range(RESPONSE_CHUNKS):
        start = r * width
        part = respond(
            guesses[r % 2], occ_parts[start // chunk], orbitals, start, start % chunk, width
        )
        for bit in orders[r % 2]:
            part = halve(part, "orb", bit, 0, jnp.bfloat16)
        owned.append(part)
    owned_sum = jnp.concatenate(owned, 1)

    row_count = points_dev // SIDE
    plane_rows = owned_sum.reshape(owned_sum.shape[0], row_count, SIDE)
    by_columns = jnp.einsum("vrc,dc->vrd", plane_rows, coul_cols, precision=lax.Precision.HIGHEST)
    mixed_rows = jnp.einsum(
        "ab,vbc->vac",
        coul_rows,
        lax.all_to_all(by_columns, "cell", split_axis=2, concat_axis=1, tiled=True),
        precision=lax.Precision.HIGHEST,
    )
    return lax.all_to_all(mixed_rows, "cell", split_axis=1, concat_axis=2, tiled=True)


def solution(mesh):
    placed = (P(None, "cell"), P("orb", "cell"), P(), P(), P(), P())
    return jax.shard_map(
        body, mesh=mesh, in_specs=placed, out_specs=P("orb", "cell", None), check_vma=False
    )
```

```python
import functools

import jax
import jax.numpy as jnp
import numpy as np
from jax import lax
from jax.experimental import pallas as pl
from jax.experimental.pallas import tpu as pltpu
from jax.sharding import PartitionSpec as P

SIDE = 256
GATHER_CHUNKS = 2
RESPONSE_CHUNKS = 4
VMEM = 56 * 1024 * 1024


def swap(x, axis, bit):
    n = lax.axis_size(axis)
    return lax.ppermute(x, axis, [(s, s ^ bit) for s in range(n)])


def upper(axis, bit):
    return (lax.axis_index(axis) // bit) % 2


def halve(x, axis, bit, dim, wire=None):
    half = x.shape[dim] // 2
    side = upper(axis, bit)
    keep = lax.dynamic_slice_in_dim(x, side * half, half, dim)
    send = lax.dynamic_slice_in_dim(x, (1 - side) * half, half, dim)
    if wire is not None:
        send = send.astype(wire)
    return keep + swap(send, axis, bit).astype(x.dtype)


def double(x, axis, bit, dim):
    other = swap(x, axis, bit)
    low = upper(axis, bit) == 0
    return jnp.concatenate([jnp.where(low, x, other), jnp.where(low, other, x)], dim)


def bits_of(axis):
    n = lax.axis_size(axis)
    return [1 << k for k in range(n.bit_length() - 1)]


def pair_rows(occ_ref, orb, first, count):
    return jnp.concatenate([occ_ref[i : i + 1, :] * orb for i in range(first, first + count)], 0)


def project_kernel(group, occ_ref, orb_ref, pot_ref, out_ref, acc):
    step = pl.program_id(0)

    @pl.when(step == 0)
    def _():
        acc[...] = jnp.zeros_like(acc)

    turned = pot_ref[...].T
    orb = orb_ref[...]
    rows = group * orb.shape[0]
    for k in range(occ_ref.shape[0] // group):
        pairs = pair_rows(occ_ref, orb, k * group, group)
        acc[k * rows : (k + 1) * rows, :] += jnp.dot(
            pairs, turned, preferred_element_type=jnp.float32
        )

    @pl.when(step == pl.num_programs(0) - 1)
    def _():
        out_ref[...] = acc[...].T


def project(occ, orbitals, potentials, start):
    slots, width = occ.shape
    stored = orbitals.shape[0]
    nv = potentials.shape[0]
    block = min(1024, width)
    shift = start // block
    pairs = slots * stored
    return pl.pallas_call(
        functools.partial(project_kernel, max(1, 256 // stored)),
        out_shape=jax.ShapeDtypeStruct((nv, pairs), jnp.float32),
        grid=(width // block,),
        in_specs=[
            pl.BlockSpec((slots, block), lambda s: (0, s)),
            pl.BlockSpec((stored, block), lambda s: (0, s + shift)),
            pl.BlockSpec((nv, block), lambda s: (0, s + shift)),
        ],
        out_specs=pl.BlockSpec((nv, pairs), lambda s: (0, 0)),
        scratch_shapes=[pltpu.VMEM((pairs, nv), jnp.float32)],
        compiler_params=pltpu.CompilerParams(vmem_limit_bytes=VMEM),
        cost_estimate=pl.CostEstimate(
            flops=2 * pairs * nv * width * 3,
            bytes_accessed=2 * width * (slots + stored + nv),
            transcendentals=0,
        ),
        name="project",
    )(occ, orbitals, potentials)


def respond_kernel(group, guess_ref, occ_ref, orb_ref, out_ref):
    orb = orb_ref[...]
    rows = group * orb.shape[0]
    total = None
    for k in range(occ_ref.shape[0] // group):
        pairs = pair_rows(occ_ref, orb, k * group, group)
        term = jnp.dot(
            guess_ref[:, k * rows : (k + 1) * rows], pairs, preferred_element_type=jnp.float32
        )
        total = term if total is None else total + term
    out_ref[...] = total


def respond(guess, occ, orbitals, start, occ_start, width):
    slots = occ.shape[0]
    stored = orbitals.shape[0]
    nv, pairs = guess.shape
    block = min(512, width)
    shift = start // block
    occ_shift = occ_start // block
    return pl.pallas_call(
        functools.partial(respond_kernel, max(1, 256 // stored)),
        out_shape=jax.ShapeDtypeStruct((nv, width), jnp.float32),
        grid=(width // block,),
        in_specs=[
            pl.BlockSpec((nv, pairs), lambda s: (0, 0)),
            pl.BlockSpec((slots, block), lambda s: (0, s + occ_shift)),
            pl.BlockSpec((stored, block), lambda s: (0, s + shift)),
        ],
        out_specs=pl.BlockSpec((nv, block), lambda s: (0, s)),
        compiler_params=pltpu.CompilerParams(vmem_limit_bytes=VMEM),
        cost_estimate=pl.CostEstimate(
            flops=2 * pairs * nv * width * 3,
            bytes_accessed=2 * width * (slots + stored) + 4 * nv * width,
            transcendentals=0,
        ),
        name="respond",
    )(guess, occ, orbitals)


def mix_kernel(mixer_ref, stack_ref, out_ref):
    out_ref[0] = jnp.dot(
        mixer_ref[...],
        stack_ref[0].astype(jnp.float32),
        precision=lax.Precision.HIGHEST,
        preferred_element_type=jnp.float32,
    )


def mix_rows(mixer, stack):
    held, total_rows, side = stack.shape
    rows = mixer.shape[0]
    return pl.pallas_call(
        mix_kernel,
        out_shape=jax.ShapeDtypeStruct((held, rows, side), jnp.float32),
        grid=(held,),
        in_specs=[
            pl.BlockSpec((rows, total_rows), lambda v: (0, 0)),
            pl.BlockSpec((1, total_rows, side), lambda v: (v, 0, 0)),
        ],
        out_specs=pl.BlockSpec((1, rows, side), lambda v: (v, 0, 0)),
        name="mix_rows",
    )(mixer, stack)


def owner_order(nv, count, order):
    per = nv // count
    owners = []
    for place in range(count):
        owner = 0
        for depth, bit in enumerate(order):
            if (place >> (len(order) - 1 - depth)) & 1:
                owner |= bit
        owners.append(owner)
    return np.concatenate([np.arange(per) + o * per for o in owners])


def program(potentials, orbitals, levels, occ_index, coul_rows, coul_cols):
    nv, points_dev = potentials.shape
    volume = points_dev * lax.axis_size("cell")
    orb_count = lax.axis_size("orb")
    my_rank = lax.axis_index("orb")
    per_orb = orbitals.shape[0]
    orb_bits = bits_of("orb")
    cell_bits = bits_of("cell")
    orders = [orb_bits, orb_bits[1:] + orb_bits[:1]]

    labels = jnp.arange(levels.shape[0], dtype=jnp.int32)
    marked = jnp.any(occ_index[:, None] == labels[None, :], axis=0)
    empty_all = 1.0 - marked.astype(jnp.float32)
    occ_hot = (occ_index[:, None] == labels[None, :]).astype(jnp.float32)
    occ_level = jnp.sum(occ_hot * levels[None, :], axis=1)
    basis_level = lax.dynamic_slice_in_dim(levels, my_rank * per_orb, per_orb)
    basis_empty = lax.dynamic_slice_in_dim(empty_all, my_rank * per_orb, per_orb)
    weights = -2.0 * basis_empty[None, :] / (occ_level[:, None] + basis_level[None, :])
    weights = (weights / volume).reshape(1, -1)

    owned_ids = my_rank * per_orb + jnp.arange(per_orb, dtype=jnp.int32)
    picker = (occ_index[:, None] == owned_ids[None, :]).astype(jnp.bfloat16)

    chunk = points_dev // GATHER_CHUNKS
    occ_parts = []
    for g in range(GATHER_CHUNKS):
        piece = jnp.dot(
            picker,
            orbitals[:, g * chunk : (g + 1) * chunk],
            preferred_element_type=jnp.float32,
        ).astype(jnp.bfloat16)
        order = orders[g % 2]
        for bit in order:
            piece = halve(piece, "orb", bit, 1)
        for bit in order[::-1]:
            piece = double(piece, "orb", bit, 1)
        occ_parts.append(piece)

    inter = None
    for g in range(GATHER_CHUNKS):
        part = project(occ_parts[g], orbitals, potentials, g * chunk)
        inter = part if inter is None else inter + part
    scale = weights
    for bit in cell_bits:
        inter = halve(inter, "cell", bit, 1)
        half = scale.shape[1] // 2
        scale = lax.dynamic_slice_in_dim(scale, upper("cell", bit) * half, half, 1)
    guess = (inter * scale).astype(jnp.bfloat16)
    for bit in cell_bits[::-1]:
        guess = double(guess, "cell", bit, 1)

    width = points_dev // RESPONSE_CHUNKS
    guesses = []
    for order in orders:
        rows = owner_order(nv, orb_count, order)
        place = jnp.asarray(rows[:, None] == np.arange(nv)[None, :], jnp.bfloat16)
        guesses.append(
            jnp.dot(place, guess, preferred_element_type=jnp.float32).astype(jnp.bfloat16)
        )
    owned = []
    for r in range(RESPONSE_CHUNKS):
        start = r * width
        part = respond(
            guesses[r % 2], occ_parts[start // chunk], orbitals, start, start % chunk, width
        )
        for bit in orders[r % 2]:
            part = halve(part, "orb", bit, 0, jnp.bfloat16)
        owned.append(part)
    owned_sum = jnp.concatenate(owned, 1)

    row_count = points_dev // SIDE
    held = owned_sum.shape[0]
    plane = jnp.dot(
        owned_sum.reshape(held * row_count, SIDE), coul_cols.T, precision=lax.Precision.HIGHEST
    )
    stack = plane.astype(jnp.bfloat16).reshape(held, row_count, SIDE)
    offsets = [0]
    for bit in cell_bits[::-1]:
        stack = jnp.concatenate([stack, swap(stack, "cell", bit)], 1)
        offsets = offsets + [o ^ bit for o in offsets]
    my_cell = lax.axis_index("cell")
    my_rows = lax.dynamic_slice_in_dim(coul_rows, my_cell * row_count, row_count, 0)
    mixer = jnp.concatenate(
        [
            lax.dynamic_slice_in_dim(my_rows, (my_cell ^ o) * row_count, row_count, 1)
            for o in offsets
        ],
        1,
    )
    return mix_rows(mixer, stack)


def solution(mesh):
    placed = (P(None, "cell"), P("orb", "cell"), P(), P(), P(), P())
    return jax.shard_map(
        program, mesh=mesh, in_specs=placed, out_specs=P("orb", "cell", None), check_vma=False
    )
```

```python
import functools

import jax
import jax.numpy as jnp
import numpy as np
from jax import lax
from jax.experimental import pallas as pl
from jax.experimental.pallas import tpu as pltpu
from jax.sharding import PartitionSpec as P

SIDE = 256
MESH = pl.DeviceIdType.MESH
RESPONSE_CHUNKS = 4
VMEM = 56 * 1024 * 1024


def swap(x, axis, bit):
    n = lax.axis_size(axis)
    return lax.ppermute(x, axis, [(s, s ^ bit) for s in range(n)])


def upper(axis, bit):
    return (lax.axis_index(axis) // bit) % 2


def halve(x, axis, bit, dim, wire=None):
    half = x.shape[dim] // 2
    side = upper(axis, bit)
    keep = lax.dynamic_slice_in_dim(x, side * half, half, dim)
    send = lax.dynamic_slice_in_dim(x, (1 - side) * half, half, dim)
    if wire is not None:
        send = send.astype(wire)
    return keep + swap(send, axis, bit).astype(x.dtype)


def double(x, axis, bit, dim):
    other = swap(x, axis, bit)
    low = upper(axis, bit) == 0
    return jnp.concatenate([jnp.where(low, x, other), jnp.where(low, other, x)], dim)


def bits_of(axis):
    n = lax.axis_size(axis)
    return [1 << k for k in range(n.bit_length() - 1)]


def pair_rows(occ_ref, orb, first, count):
    return jnp.concatenate([occ_ref[i : i + 1, :] * orb for i in range(first, first + count)], 0)


def partner_of(axis, bit):
    me = lax.axis_index(axis)
    return me + bit - 2 * bit * ((me // bit) % 2)


def greet(axis, bits):
    barrier = pltpu.get_barrier_semaphore()
    for bit in bits:
        pl.semaphore_signal(
            barrier, inc=1, device_id={axis: partner_of(axis, bit)}, device_id_type=MESH
        )
    pl.semaphore_wait(barrier, len(bits))


def project_block(group, at, block, occ_ref, orb_ref, pot_ref, acc):
    turned = pot_ref[:, pl.ds(at, block)].T
    orb = orb_ref[:, pl.ds(at, block)]
    rows = group * orb.shape[0]
    for k in range(occ_ref.shape[0] // group):
        pairs = jnp.concatenate(
            [
                occ_ref[i : i + 1, pl.ds(at, block)] * orb
                for i in range(k * group, (k + 1) * group)
            ],
            0,
        )
        acc[k * rows : (k + 1) * rows, :] += jnp.dot(
            pairs, turned, preferred_element_type=jnp.float32
        )


def gather_kernel(bits, chunks, group, picker, orb, pot, occ, inter, work, land, acc, sent, came):
    points = orb.shape[1]
    chunk = points // chunks
    depth = len(bits)
    block = min(1024, chunk)
    orders = [bits, bits[1:] + bits[:1]]
    place = [c * chunk for c in range(chunks)]
    flying = [None] * chunks

    def push(c, step, src, dst, bit):
        copy = pltpu.make_async_remote_copy(
            src_ref=src,
            dst_ref=dst,
            send_sem=sent.at[c, step],
            recv_sem=came.at[c, step],
            device_id={"orb": partner_of("orb", bit)},
            device_id_type=MESH,
        )
        copy.start()
        flying[c] = copy

    def advance(c, step):
        order = orders[c % 2]
        if step == 0:
            span = slice(c * chunk, (c + 1) * chunk)
            work[:, span] = jnp.dot(
                picker[...], orb[:, span], preferred_element_type=jnp.float32
            ).astype(work.dtype)
        else:
            flying[c].wait()
            if step <= depth:
                size = chunk >> step
                here = pl.ds(pl.multiple_of(place[c], 128), size)
                base = c * chunk + chunk - (chunk >> (step - 1))
                total = work[:, here] + land[:, base : base + size]
                if step < depth:
                    work[:, here] = total
                else:
                    occ[:, here] = total
            else:
                size = chunk >> (2 * depth - step + 1)
                bit = order[2 * depth - step]
                place[c] = place[c] - upper("orb", bit) * size
        if step < depth:
            bit = order[step]
            half = chunk >> (step + 1)
            side = upper("orb", bit)
            away = pl.multiple_of(place[c] + (1 - side) * half, 128)
            base = c * chunk + chunk - (chunk >> step)
            push(c, step, work.at[:, pl.ds(away, half)], land.at[:, pl.ds(base, half)], bit)
            place[c] = place[c] + side * half
        elif step < 2 * depth:
            size = chunk >> (2 * depth - step)
            here = pl.ds(pl.multiple_of(place[c], 128), size)
            push(c, step, occ.at[:, here], occ.at[:, here], order[2 * depth - 1 - step])

    acc[...] = jnp.zeros_like(acc)
    greet("orb", bits)
    teams = [list(range(t, min(t + 2, chunks))) for t in range(0, chunks, 2)]
    for tick in range(2 * depth + len(teams)):
        for t, team in enumerate(teams):
            step = tick - t
            if 0 <= step <= 2 * depth:
                for c in team:
                    advance(c, step)
        done = tick - 2 * depth
        if 0 <= done < len(teams):
            team = teams[done]
            first = team[0] * chunk // block

            @pl.loop(first, first + len(team) * chunk // block)
            def _(b):
                at = pl.multiple_of(b * block, block)
                project_block(group, at, block, occ, orb, pot, acc)

    inter[...] = acc[...].T


def gather_project(picker, orbitals, potentials):
    stored, points = orbitals.shape
    slots = picker.shape[0]
    nv = potentials.shape[0]
    pairs = slots * stored
    bits = bits_of("orb")
    chunks = max(1, min(8, points // (128 << len(bits))))
    steps = 2 * len(bits)
    return pl.pallas_call(
        functools.partial(gather_kernel, bits, chunks, max(1, 256 // stored)),
        out_shape=(
            jax.ShapeDtypeStruct((slots, points), jnp.bfloat16),
            jax.ShapeDtypeStruct((nv, pairs), jnp.float32),
        ),
        in_specs=[pl.BlockSpec(memory_space=pltpu.VMEM)] * 3,
        out_specs=(pl.BlockSpec(memory_space=pltpu.VMEM),) * 2,
        scratch_shapes=[
            pltpu.VMEM((slots, points), jnp.bfloat16),
            pltpu.VMEM((slots, points), jnp.bfloat16),
            pltpu.VMEM((pairs, nv), jnp.float32),
            pltpu.SemaphoreType.DMA((chunks, steps)),
            pltpu.SemaphoreType.DMA((chunks, steps)),
        ],
        compiler_params=pltpu.CompilerParams(
            vmem_limit_bytes=VMEM, collective_id=0, has_side_effects=True
        ),
        name="gather_project",
    )(picker, orbitals, potentials)


def respond_kernel(group, guess_ref, occ_ref, orb_ref, out_ref):
    orb = orb_ref[...]
    rows = group * orb.shape[0]
    total = None
    for k in range(occ_ref.shape[0] // group):
        pairs = pair_rows(occ_ref, orb, k * group, group)
        term = jnp.dot(
            guess_ref[:, k * rows : (k + 1) * rows], pairs, preferred_element_type=jnp.float32
        )
        total = term if total is None else total + term
    out_ref[...] = total


def respond(guess, occ, orbitals, start, occ_start, width):
    slots = occ.shape[0]
    stored = orbitals.shape[0]
    nv, pairs = guess.shape
    block = min(512, width)
    shift = start // block
    occ_shift = occ_start // block
    return pl.pallas_call(
        functools.partial(respond_kernel, max(1, 256 // stored)),
        out_shape=jax.ShapeDtypeStruct((nv, width), jnp.float32),
        grid=(width // block,),
        in_specs=[
            pl.BlockSpec((nv, pairs), lambda s: (0, 0)),
            pl.BlockSpec((slots, block), lambda s: (0, s + occ_shift)),
            pl.BlockSpec((stored, block), lambda s: (0, s + shift)),
        ],
        out_specs=pl.BlockSpec((nv, block), lambda s: (0, s)),
        compiler_params=pltpu.CompilerParams(vmem_limit_bytes=VMEM),
        cost_estimate=pl.CostEstimate(
            flops=2 * pairs * nv * width * 3,
            bytes_accessed=2 * width * (slots + stored) + 4 * nv * width,
            transcendentals=0,
        ),
        name="respond",
    )(guess, occ, orbitals)


def mix_kernel(mixer_ref, stack_ref, out_ref):
    out_ref[0] = jnp.dot(
        mixer_ref[...],
        stack_ref[0].astype(jnp.float32),
        precision=lax.Precision.HIGHEST,
        preferred_element_type=jnp.float32,
    )


def mix_rows(mixer, stack):
    held, total_rows, side = stack.shape
    rows = mixer.shape[0]
    return pl.pallas_call(
        mix_kernel,
        out_shape=jax.ShapeDtypeStruct((held, rows, side), jnp.float32),
        grid=(held,),
        in_specs=[
            pl.BlockSpec((rows, total_rows), lambda v: (0, 0)),
            pl.BlockSpec((1, total_rows, side), lambda v: (v, 0, 0)),
        ],
        out_specs=pl.BlockSpec((1, rows, side), lambda v: (v, 0, 0)),
        name="mix_rows",
    )(mixer, stack)


def owner_order(nv, count, order):
    per = nv // count
    owners = []
    for place in range(count):
        owner = 0
        for depth, bit in enumerate(order):
            if (place >> (len(order) - 1 - depth)) & 1:
                owner |= bit
        owners.append(owner)
    return np.concatenate([np.arange(per) + o * per for o in owners])


def program(potentials, orbitals, levels, occ_index, coul_rows, coul_cols):
    nv, points_dev = potentials.shape
    volume = points_dev * lax.axis_size("cell")
    orb_count = lax.axis_size("orb")
    my_rank = lax.axis_index("orb")
    per_orb = orbitals.shape[0]
    orb_bits = bits_of("orb")
    cell_bits = bits_of("cell")
    orders = [orb_bits, orb_bits[1:] + orb_bits[:1]]

    labels = jnp.arange(levels.shape[0], dtype=jnp.int32)
    marked = jnp.any(occ_index[:, None] == labels[None, :], axis=0)
    empty_all = 1.0 - marked.astype(jnp.float32)
    occ_hot = (occ_index[:, None] == labels[None, :]).astype(jnp.float32)
    occ_level = jnp.sum(occ_hot * levels[None, :], axis=1)
    basis_level = lax.dynamic_slice_in_dim(levels, my_rank * per_orb, per_orb)
    basis_empty = lax.dynamic_slice_in_dim(empty_all, my_rank * per_orb, per_orb)
    weights = -2.0 * basis_empty[None, :] / (occ_level[:, None] + basis_level[None, :])
    weights = (weights / volume).reshape(1, -1)

    owned_ids = my_rank * per_orb + jnp.arange(per_orb, dtype=jnp.int32)
    picker = (occ_index[:, None] == owned_ids[None, :]).astype(jnp.bfloat16)

    occ, inter = gather_project(picker, orbitals, potentials)
    scale = weights
    for bit in cell_bits:
        inter = halve(inter, "cell", bit, 1)
        half = scale.shape[1] // 2
        scale = lax.dynamic_slice_in_dim(scale, upper("cell", bit) * half, half, 1)
    guess = (inter * scale).astype(jnp.bfloat16)
    for bit in cell_bits[::-1]:
        guess = double(guess, "cell", bit, 1)

    width = points_dev // RESPONSE_CHUNKS
    guesses = []
    for order in orders:
        rows = owner_order(nv, orb_count, order)
        place = jnp.asarray(rows[:, None] == np.arange(nv)[None, :], jnp.bfloat16)
        guesses.append(
            jnp.dot(place, guess, preferred_element_type=jnp.float32).astype(jnp.bfloat16)
        )
    owned = []
    for r in range(RESPONSE_CHUNKS):
        start = r * width
        part = respond(
            guesses[r % 2], occ, orbitals, start, start, width
        )
        for bit in orders[r % 2]:
            part = halve(part, "orb", bit, 0, jnp.bfloat16)
        owned.append(part)
    owned_sum = jnp.concatenate(owned, 1)

    row_count = points_dev // SIDE
    held = owned_sum.shape[0]
    plane = jnp.dot(
        owned_sum.reshape(held * row_count, SIDE), coul_cols.T, precision=lax.Precision.HIGHEST
    )
    stack = plane.astype(jnp.bfloat16).reshape(held, row_count, SIDE)
    offsets = [0]
    for bit in cell_bits[::-1]:
        stack = jnp.concatenate([stack, swap(stack, "cell", bit)], 1)
        offsets = offsets + [o ^ bit for o in offsets]
    my_cell = lax.axis_index("cell")
    my_rows = lax.dynamic_slice_in_dim(coul_rows, my_cell * row_count, row_count, 0)
    mixer = jnp.concatenate(
        [
            lax.dynamic_slice_in_dim(my_rows, (my_cell ^ o) * row_count, row_count, 1)
            for o in offsets
        ],
        1,
    )
    return mix_rows(mixer, stack)


def solution(mesh):
    placed = (P(None, "cell"), P("orb", "cell"), P(), P(), P(), P())
    return jax.shard_map(
        program, mesh=mesh, in_specs=placed, out_specs=P("orb", "cell", None), check_vma=False
    )
```

```python
import functools

import jax
import jax.numpy as jnp
import numpy as np
from jax import lax
from jax.experimental import pallas as pl
from jax.experimental.pallas import tpu as pltpu
from jax.sharding import PartitionSpec as P

SIDE = 256
MESH = pl.DeviceIdType.MESH
VMEM = 56 * 1024 * 1024


def swap(x, axis, bit):
    n = lax.axis_size(axis)
    return lax.ppermute(x, axis, [(s, s ^ bit) for s in range(n)])


def upper(axis, bit):
    return (lax.axis_index(axis) // bit) % 2


def halve(x, axis, bit, dim, wire=None):
    half = x.shape[dim] // 2
    side = upper(axis, bit)
    keep = lax.dynamic_slice_in_dim(x, side * half, half, dim)
    send = lax.dynamic_slice_in_dim(x, (1 - side) * half, half, dim)
    if wire is not None:
        send = send.astype(wire)
    return keep + swap(send, axis, bit).astype(x.dtype)


def double(x, axis, bit, dim):
    other = swap(x, axis, bit)
    low = upper(axis, bit) == 0
    return jnp.concatenate([jnp.where(low, x, other), jnp.where(low, other, x)], dim)


def bits_of(axis):
    n = lax.axis_size(axis)
    return [1 << k for k in range(n.bit_length() - 1)]


def partner_of(axis, bit):
    me = lax.axis_index(axis)
    return me + bit - 2 * bit * ((me // bit) % 2)


def greet(axis, bits):
    barrier = pltpu.get_barrier_semaphore()
    for bit in bits:
        pl.semaphore_signal(
            barrier, inc=1, device_id={axis: partner_of(axis, bit)}, device_id_type=MESH
        )
    pl.semaphore_wait(barrier, len(bits))


def project_block(group, at, block, occ_ref, orb_ref, pot_ref, acc):
    turned = pot_ref[:, pl.ds(at, block)].T
    orb = orb_ref[:, pl.ds(at, block)]
    rows = group * orb.shape[0]
    for k in range(occ_ref.shape[0] // group):
        pairs = jnp.concatenate(
            [
                occ_ref[i : i + 1, pl.ds(at, block)] * orb
                for i in range(k * group, (k + 1) * group)
            ],
            0,
        )
        acc[k * rows : (k + 1) * rows, :] += jnp.dot(
            pairs, turned, preferred_element_type=jnp.float32
        )


def gather_kernel(bits, chunks, group, picker, orb, pot, occ, inter, work, land, acc, sent, came):
    points = orb.shape[1]
    chunk = points // chunks
    depth = len(bits)
    block = min(1024, chunk)
    orders = [bits, bits[1:] + bits[:1]]
    place = [c * chunk for c in range(chunks)]
    flying = [None] * chunks

    def push(c, step, src, dst, bit):
        copy = pltpu.make_async_remote_copy(
            src_ref=src,
            dst_ref=dst,
            send_sem=sent.at[c, step],
            recv_sem=came.at[c, step],
            device_id={"orb": partner_of("orb", bit)},
            device_id_type=MESH,
        )
        copy.start()
        flying[c] = copy

    def advance(c, step):
        order = orders[c % 2]
        if step == 0:
            span = slice(c * chunk, (c + 1) * chunk)
            work[:, span] = jnp.dot(
                picker[...], orb[:, span], preferred_element_type=jnp.float32
            ).astype(work.dtype)
        else:
            flying[c].wait()
            if step <= depth:
                size = chunk >> step
                here = pl.ds(pl.multiple_of(place[c], 128), size)
                base = c * chunk + chunk - (chunk >> (step - 1))
                total = work[:, here] + land[:, base : base + size]
                if step < depth:
                    work[:, here] = total
                else:
                    occ[:, here] = total
            else:
                size = chunk >> (2 * depth - step + 1)
                bit = order[2 * depth - step]
                place[c] = place[c] - upper("orb", bit) * size
        if step < depth:
            bit = order[step]
            half = chunk >> (step + 1)
            side = upper("orb", bit)
            away = pl.multiple_of(place[c] + (1 - side) * half, 128)
            base = c * chunk + chunk - (chunk >> step)
            push(c, step, work.at[:, pl.ds(away, half)], land.at[:, pl.ds(base, half)], bit)
            place[c] = place[c] + side * half
        elif step < 2 * depth:
            size = chunk >> (2 * depth - step)
            here = pl.ds(pl.multiple_of(place[c], 128), size)
            push(c, step, occ.at[:, here], occ.at[:, here], order[2 * depth - 1 - step])

    acc[...] = jnp.zeros_like(acc)
    greet("orb", bits)
    teams = [list(range(t, min(t + 2, chunks))) for t in range(0, chunks, 2)]
    for tick in range(2 * depth + len(teams)):
        for t, team in enumerate(teams):
            step = tick - t
            if 0 <= step <= 2 * depth:
                for c in team:
                    advance(c, step)
        done = tick - 2 * depth
        if 0 <= done < len(teams):
            team = teams[done]
            first = team[0] * chunk // block

            @pl.loop(first, first + len(team) * chunk // block)
            def _(b):
                at = pl.multiple_of(b * block, block)
                project_block(group, at, block, occ, orb, pot, acc)

    inter[...] = acc[...].T


def gather_project(picker, orbitals, potentials):
    stored, points = orbitals.shape
    slots = picker.shape[0]
    nv = potentials.shape[0]
    pairs = slots * stored
    bits = bits_of("orb")
    chunks = max(1, min(8, points // (128 << len(bits))))
    steps = 2 * len(bits)
    return pl.pallas_call(
        functools.partial(gather_kernel, bits, chunks, max(1, 256 // stored)),
        out_shape=(
            jax.ShapeDtypeStruct((slots, points), jnp.bfloat16),
            jax.ShapeDtypeStruct((nv, pairs), jnp.float32),
        ),
        in_specs=[pl.BlockSpec(memory_space=pltpu.VMEM)] * 3,
        out_specs=(pl.BlockSpec(memory_space=pltpu.VMEM),) * 2,
        scratch_shapes=[
            pltpu.VMEM((slots, points), jnp.bfloat16),
            pltpu.VMEM((slots, points), jnp.bfloat16),
            pltpu.VMEM((pairs, nv), jnp.float32),
            pltpu.SemaphoreType.DMA((chunks, steps)),
            pltpu.SemaphoreType.DMA((chunks, steps)),
        ],
        compiler_params=pltpu.CompilerParams(
            vmem_limit_bytes=VMEM, collective_id=0, has_side_effects=True
        ),
        name="gather_project",
    )(picker, orbitals, potentials)


def respond_kernel(bits, chunks, group, *refs):
    depth = len(bits)
    guess_refs, (occ, orb, out), rest = refs[:2], refs[2:5], refs[5:]
    keeps, sends, lands = rest[:depth], rest[depth : 2 * depth], rest[2 * depth : 3 * depth]
    sent, came = rest[3 * depth :]
    points = orb.shape[1]
    chunk = points // chunks
    block = min(512, chunk)
    orders = [bits, bits[1:] + bits[:1]]
    flying = [None] * chunks

    def split(value, bit, step, span):
        half = value.shape[0] // 2
        low, high = value[:half], value[half:]
        at_low = upper("orb", bit) == 0
        keeps[step][:, span] = jnp.where(at_low, low, high)
        sends[step][:, span] = jnp.where(at_low, high, low).astype(sends[step].dtype)

    def push(c, step):
        span = pl.ds(c * chunk, chunk)
        copy = pltpu.make_async_remote_copy(
            src_ref=sends[step].at[:, span],
            dst_ref=lands[step].at[:, span],
            send_sem=sent.at[c, step],
            recv_sem=came.at[c, step],
            device_id={"orb": partner_of("orb", orders[c % 2][step])},
            device_id_type=MESH,
        )
        copy.start()
        flying[c] = copy

    def compute(c):
        guess = guess_refs[c % 2]

        @pl.loop(0, chunk // block)
        def _(b):
            span = pl.ds(pl.multiple_of(c * chunk + b * block, block), block)
            basis = orb[:, span]
            rows = group * basis.shape[0]
            total = None
            for k in range(occ.shape[0] // group):
                pairs = jnp.concatenate(
                    [occ[i : i + 1, span] * basis for i in range(k * group, (k + 1) * group)], 0
                )
                term = jnp.dot(
                    guess[:, k * rows : (k + 1) * rows], pairs, preferred_element_type=jnp.float32
                )
                total = term if total is None else total + term
            split(total, orders[c % 2][0], 0, span)

    def advance(c, step):
        flying[c].wait()
        span = pl.ds(c * chunk, chunk)
        value = keeps[step - 1][:, span] + lands[step - 1][:, span].astype(jnp.float32)
        if step == depth:
            out[:, span] = value
        else:
            split(value, orders[c % 2][step], step, span)
            push(c, step)

    greet("orb", bits)
    lag = 2
    for tick in range(chunks + lag * depth):
        if tick < chunks:
            compute(tick)
            push(tick, 0)
        for step in range(1, depth + 1):
            c = tick - lag * step
            if 0 <= c < chunks:
                advance(c, step)


def respond(guesses, occ, orbitals):
    _, points = occ.shape
    stored = orbitals.shape[0]
    nv, _ = guesses[0].shape
    bits = bits_of("orb")
    chunks = max(1, min(16, points // 512))
    sizes = [nv >> (k + 1) for k in range(len(bits))]
    return pl.pallas_call(
        functools.partial(respond_kernel, bits, chunks, max(1, 256 // stored)),
        out_shape=jax.ShapeDtypeStruct((nv >> len(bits), points), jnp.float32),
        in_specs=[pl.BlockSpec(memory_space=pltpu.VMEM)] * 4,
        out_specs=pl.BlockSpec(memory_space=pltpu.VMEM),
        scratch_shapes=[pltpu.VMEM((n, points), jnp.float32) for n in sizes]
        + [pltpu.VMEM((n, points), jnp.bfloat16) for n in sizes] * 2
        + [pltpu.SemaphoreType.DMA((chunks, len(bits)))] * 2,
        compiler_params=pltpu.CompilerParams(
            vmem_limit_bytes=VMEM, collective_id=1, has_side_effects=True
        ),
        name="respond",
    )(*guesses, occ, orbitals)


def mix_kernel(mixer_ref, stack_ref, out_ref):
    out_ref[0] = jnp.dot(
        mixer_ref[...],
        stack_ref[0].astype(jnp.float32),
        precision=lax.Precision.HIGHEST,
        preferred_element_type=jnp.float32,
    )


def mix_rows(mixer, stack):
    held, total_rows, side = stack.shape
    rows = mixer.shape[0]
    return pl.pallas_call(
        mix_kernel,
        out_shape=jax.ShapeDtypeStruct((held, rows, side), jnp.float32),
        grid=(held,),
        in_specs=[
            pl.BlockSpec((rows, total_rows), lambda v: (0, 0)),
            pl.BlockSpec((1, total_rows, side), lambda v: (v, 0, 0)),
        ],
        out_specs=pl.BlockSpec((1, rows, side), lambda v: (v, 0, 0)),
        name="mix_rows",
    )(mixer, stack)


def owner_order(nv, count, order):
    per = nv // count
    owners = []
    for place in range(count):
        owner = 0
        for depth, bit in enumerate(order):
            if (place >> (len(order) - 1 - depth)) & 1:
                owner |= bit
        owners.append(owner)
    return np.concatenate([np.arange(per) + o * per for o in owners])


def program(potentials, orbitals, levels, occ_index, coul_rows, coul_cols):
    nv, points_dev = potentials.shape
    volume = points_dev * lax.axis_size("cell")
    orb_count = lax.axis_size("orb")
    my_rank = lax.axis_index("orb")
    per_orb = orbitals.shape[0]
    orb_bits = bits_of("orb")
    cell_bits = bits_of("cell")
    orders = [orb_bits, orb_bits[1:] + orb_bits[:1]]

    labels = jnp.arange(levels.shape[0], dtype=jnp.int32)
    marked = jnp.any(occ_index[:, None] == labels[None, :], axis=0)
    empty_all = 1.0 - marked.astype(jnp.float32)
    occ_hot = (occ_index[:, None] == labels[None, :]).astype(jnp.float32)
    occ_level = jnp.sum(occ_hot * levels[None, :], axis=1)
    basis_level = lax.dynamic_slice_in_dim(levels, my_rank * per_orb, per_orb)
    basis_empty = lax.dynamic_slice_in_dim(empty_all, my_rank * per_orb, per_orb)
    weights = -2.0 * basis_empty[None, :] / (occ_level[:, None] + basis_level[None, :])
    weights = (weights / volume).reshape(1, -1)

    owned_ids = my_rank * per_orb + jnp.arange(per_orb, dtype=jnp.int32)
    picker = (occ_index[:, None] == owned_ids[None, :]).astype(jnp.bfloat16)

    occ, inter = gather_project(picker, orbitals, potentials)
    scale = weights
    for bit in cell_bits:
        inter = halve(inter, "cell", bit, 1)
        half = scale.shape[1] // 2
        scale = lax.dynamic_slice_in_dim(scale, upper("cell", bit) * half, half, 1)
    guess = (inter * scale).astype(jnp.bfloat16)
    for bit in cell_bits[::-1]:
        guess = double(guess, "cell", bit, 1)

    guesses = []
    for order in orders:
        rows = owner_order(nv, orb_count, order)
        place = jnp.asarray(rows[:, None] == np.arange(nv)[None, :], jnp.bfloat16)
        guesses.append(
            jnp.dot(place, guess, preferred_element_type=jnp.float32).astype(jnp.bfloat16)
        )
    owned_sum = respond(guesses, occ, orbitals)

    row_count = points_dev // SIDE
    held = owned_sum.shape[0]
    plane = jnp.dot(
        owned_sum.reshape(held * row_count, SIDE), coul_cols.T, precision=lax.Precision.HIGHEST
    )
    stack = plane.astype(jnp.bfloat16).reshape(held, row_count, SIDE)
    offsets = [0]
    for bit in cell_bits[::-1]:
        stack = jnp.concatenate([stack, swap(stack, "cell", bit)], 1)
        offsets = offsets + [o ^ bit for o in offsets]
    my_cell = lax.axis_index("cell")
    my_rows = lax.dynamic_slice_in_dim(coul_rows, my_cell * row_count, row_count, 0)
    mixer = jnp.concatenate(
        [
            lax.dynamic_slice_in_dim(my_rows, (my_cell ^ o) * row_count, row_count, 1)
            for o in offsets
        ],
        1,
    )
    return mix_rows(mixer, stack)


def solution(mesh):
    placed = (P(None, "cell"), P("orb", "cell"), P(), P(), P(), P())
    return jax.shard_map(
        program, mesh=mesh, in_specs=placed, out_specs=P("orb", "cell", None), check_vma=False
    )
```

```python
import functools

import jax
import jax.numpy as jnp
import numpy as np
from jax import lax
from jax.experimental import pallas as pl
from jax.experimental.pallas import tpu as pltpu
from jax.sharding import PartitionSpec as P

SIDE = 256
MESH = pl.DeviceIdType.MESH
VMEM = 56 * 1024 * 1024


def swap(x, axis, bit):
    n = lax.axis_size(axis)
    return lax.ppermute(x, axis, [(s, s ^ bit) for s in range(n)])


def upper(axis, bit):
    return (lax.axis_index(axis) // bit) % 2


def halve(x, axis, bit, dim, wire=None):
    half = x.shape[dim] // 2
    side = upper(axis, bit)
    keep = lax.dynamic_slice_in_dim(x, side * half, half, dim)
    send = lax.dynamic_slice_in_dim(x, (1 - side) * half, half, dim)
    if wire is not None:
        send = send.astype(wire)
    return keep + swap(send, axis, bit).astype(x.dtype)


def double(x, axis, bit, dim):
    other = swap(x, axis, bit)
    low = upper(axis, bit) == 0
    return jnp.concatenate([jnp.where(low, x, other), jnp.where(low, other, x)], dim)


def bits_of(axis):
    n = lax.axis_size(axis)
    return [1 << k for k in range(n.bit_length() - 1)]


def partner_of(axis, bit):
    me = lax.axis_index(axis)
    return me + bit - 2 * bit * ((me // bit) % 2)


def greet(axis, bits):
    barrier = pltpu.get_barrier_semaphore()
    for bit in bits:
        pl.semaphore_signal(
            barrier, inc=1, device_id={axis: partner_of(axis, bit)}, device_id_type=MESH
        )
    pl.semaphore_wait(barrier, len(bits))


def project_block(group, at, block, occ_ref, orb_ref, pot_ref, acc):
    turned = pot_ref[:, pl.ds(at, block)].T
    orb = orb_ref[:, pl.ds(at, block)]
    rows = group * orb.shape[0]
    for k in range(occ_ref.shape[0] // group):
        pairs = jnp.concatenate(
            [
                occ_ref[i : i + 1, pl.ds(at, block)] * orb
                for i in range(k * group, (k + 1) * group)
            ],
            0,
        )
        acc[k * rows : (k + 1) * rows, :] += jnp.dot(
            pairs, turned, preferred_element_type=jnp.float32
        )


def gather_kernel(bits, chunks, group, picker, orb, pot, occ, inter, work, land, acc, sent, came):
    points = orb.shape[1]
    chunk = points // chunks
    depth = len(bits)
    block = min(1024, chunk)
    orders = [bits, bits[1:] + bits[:1]]
    place = [c * chunk for c in range(chunks)]
    flying = [None] * chunks

    def push(c, step, src, dst, bit):
        copy = pltpu.make_async_remote_copy(
            src_ref=src,
            dst_ref=dst,
            send_sem=sent.at[c, step],
            recv_sem=came.at[c, step],
            device_id={"orb": partner_of("orb", bit)},
            device_id_type=MESH,
        )
        copy.start()
        flying[c] = copy

    def advance(c, step):
        order = orders[c % 2]
        if step == 0:
            span = slice(c * chunk, (c + 1) * chunk)
            work[:, span] = jnp.dot(
                picker[...], orb[:, span], preferred_element_type=jnp.float32
            ).astype(work.dtype)
        else:
            flying[c].wait()
            if step <= depth:
                size = chunk >> step
                here = pl.ds(pl.multiple_of(place[c], 128), size)
                base = c * chunk + chunk - (chunk >> (step - 1))
                total = work[:, here] + land[:, base : base + size]
                if step < depth:
                    work[:, here] = total
                else:
                    occ[:, here] = total
            else:
                size = chunk >> (2 * depth - step + 1)
                bit = order[2 * depth - step]
                place[c] = place[c] - upper("orb", bit) * size
        if step < depth:
            bit = order[step]
            half = chunk >> (step + 1)
            side = upper("orb", bit)
            away = pl.multiple_of(place[c] + (1 - side) * half, 128)
            base = c * chunk + chunk - (chunk >> step)
            push(c, step, work.at[:, pl.ds(away, half)], land.at[:, pl.ds(base, half)], bit)
            place[c] = place[c] + side * half
        elif step < 2 * depth:
            size = chunk >> (2 * depth - step)
            here = pl.ds(pl.multiple_of(place[c], 128), size)
            push(c, step, occ.at[:, here], occ.at[:, here], order[2 * depth - 1 - step])

    acc[...] = jnp.zeros_like(acc)
    greet("orb", bits)
    teams = [list(range(t, min(t + 2, chunks))) for t in range(0, chunks, 2)]
    for tick in range(2 * depth + len(teams)):
        for t, team in enumerate(teams):
            step = tick - t
            if 0 <= step <= 2 * depth:
                for c in team:
                    advance(c, step)
        done = tick - 2 * depth
        if 0 <= done < len(teams):
            team = teams[done]
            first = team[0] * chunk // block

            @pl.loop(first, first + len(team) * chunk // block)
            def _(b):
                at = pl.multiple_of(b * block, block)
                project_block(group, at, block, occ, orb, pot, acc)

    inter[...] = acc[...].T


def gather_project(picker, orbitals, potentials):
    stored, points = orbitals.shape
    slots = picker.shape[0]
    nv = potentials.shape[0]
    pairs = slots * stored
    bits = bits_of("orb")
    chunks = max(1, min(16, points // (128 << len(bits))))
    steps = 2 * len(bits)
    return pl.pallas_call(
        functools.partial(gather_kernel, bits, chunks, max(1, 256 // stored)),
        out_shape=(
            jax.ShapeDtypeStruct((slots, points), jnp.bfloat16),
            jax.ShapeDtypeStruct((nv, pairs), jnp.float32),
        ),
        in_specs=[pl.BlockSpec(memory_space=pltpu.VMEM)] * 3,
        out_specs=(pl.BlockSpec(memory_space=pltpu.VMEM),) * 2,
        scratch_shapes=[
            pltpu.VMEM((slots, points), jnp.bfloat16),
            pltpu.VMEM((slots, points), jnp.bfloat16),
            pltpu.VMEM((pairs, nv), jnp.float32),
            pltpu.SemaphoreType.DMA((chunks, steps)),
            pltpu.SemaphoreType.DMA((chunks, steps)),
        ],
        compiler_params=pltpu.CompilerParams(
            vmem_limit_bytes=VMEM, collective_id=0, has_side_effects=True
        ),
        name="gather_project",
    )(picker, orbitals, potentials)


def respond_kernel(bits, chunks, group, *refs):
    depth = len(bits)
    (both, occ, orb, out), rest = refs[:4], refs[4:]
    nv = both.shape[0] // 2
    keeps, sends, lands = rest[:depth], rest[depth : 2 * depth], rest[2 * depth : 3 * depth]
    sent, came = rest[3 * depth :]
    points = orb.shape[1]
    chunk = points // chunks
    block = min(512, chunk)
    orders = [bits, bits[1:] + bits[:1]]
    flying = [None] * chunks

    def split(value, bit, step, span):
        half = value.shape[0] // 2
        low, high = value[:half], value[half:]
        at_low = upper("orb", bit) == 0
        keeps[step][:, span] = jnp.where(at_low, low, high)
        sends[step][:, span] = jnp.where(at_low, high, low).astype(sends[step].dtype)

    def push(c, step):
        span = pl.ds(c * chunk, chunk)
        copy = pltpu.make_async_remote_copy(
            src_ref=sends[step].at[:, span],
            dst_ref=lands[step].at[:, span],
            send_sem=sent.at[c, step],
            recv_sem=came.at[c, step],
            device_id={"orb": partner_of("orb", orders[c % 2][step])},
            device_id_type=MESH,
        )
        copy.start()
        flying[c] = copy

    def compute(c):
        mine = slice((c % 2) * nv, (c % 2 + 1) * nv)

        @pl.loop(0, chunk // block)
        def _(b):
            span = pl.ds(pl.multiple_of(c * chunk + b * block, block), block)
            basis = orb[:, span]
            rows = group * basis.shape[0]
            total = None
            for k in range(occ.shape[0] // group):
                pairs = jnp.concatenate(
                    [occ[i : i + 1, span] * basis for i in range(k * group, (k + 1) * group)], 0
                )
                term = jnp.dot(
                    both[mine, k * rows : (k + 1) * rows],
                    pairs,
                    preferred_element_type=jnp.float32,
                )
                total = term if total is None else total + term
            split(total, orders[c % 2][0], 0, span)

    def advance(c, step):
        flying[c].wait()
        span = pl.ds(c * chunk, chunk)
        value = keeps[step - 1][:, span] + lands[step - 1][:, span].astype(jnp.float32)
        if step == depth:
            out[:, span] = value
        else:
            split(value, orders[c % 2][step], step, span)
            push(c, step)

    greet("orb", bits)
    lag = 2
    for tick in range(chunks + lag * depth):
        if tick < chunks:
            compute(tick)
            push(tick, 0)
        for step in range(1, depth + 1):
            c = tick - lag * step
            if 0 <= c < chunks:
                advance(c, step)


def respond(both, occ, orbitals):
    _, points = occ.shape
    stored = orbitals.shape[0]
    nv = both.shape[0] // 2
    bits = bits_of("orb")
    chunks = max(1, min(16, points // 512))
    sizes = [nv >> (k + 1) for k in range(len(bits))]
    return pl.pallas_call(
        functools.partial(respond_kernel, bits, chunks, max(1, 256 // stored)),
        out_shape=jax.ShapeDtypeStruct((nv >> len(bits), points), jnp.float32),
        in_specs=[pl.BlockSpec(memory_space=pltpu.VMEM)] * 3,
        out_specs=pl.BlockSpec(memory_space=pltpu.VMEM),
        scratch_shapes=[pltpu.VMEM((n, points), jnp.float32) for n in sizes]
        + [pltpu.VMEM((n, points), jnp.bfloat16) for n in sizes] * 2
        + [pltpu.SemaphoreType.DMA((chunks, len(bits)))] * 2,
        compiler_params=pltpu.CompilerParams(
            vmem_limit_bytes=VMEM, collective_id=1, has_side_effects=True
        ),
        name="respond",
    )(both, occ, orbitals)


def mix_kernel(mixer_ref, stack_ref, out_ref, terms):
    rows = mixer_ref.shape[0]

    @pl.when(pl.program_id(0) == 0)
    def _():
        left = mixer_ref[...]
        for t in range(3):
            term = left.astype(jnp.bfloat16)
            terms[t * rows : (t + 1) * rows, :] = term
            left = left - term.astype(jnp.float32)

    for v in range(stack_ref.shape[0]):
        mixed = jnp.dot(terms[...], stack_ref[v], preferred_element_type=jnp.float32)
        out_ref[v] = mixed[:rows] + (mixed[rows : 2 * rows] + mixed[2 * rows :])


def mix_rows(mixer, stack):
    held, total_rows, side = stack.shape
    rows = mixer.shape[0]
    batch = 4 if held % 4 == 0 else 1
    return pl.pallas_call(
        mix_kernel,
        out_shape=jax.ShapeDtypeStruct((held, rows, side), jnp.float32),
        grid=(held // batch,),
        in_specs=[
            pl.BlockSpec((rows, total_rows), lambda v: (0, 0)),
            pl.BlockSpec((batch, total_rows, side), lambda v: (v, 0, 0)),
        ],
        out_specs=pl.BlockSpec((batch, rows, side), lambda v: (v, 0, 0)),
        scratch_shapes=[pltpu.VMEM((3 * rows, total_rows), jnp.bfloat16)],
        name="mix_rows",
    )(mixer, stack)


def owner_order(nv, count, order):
    per = nv // count
    owners = []
    for place in range(count):
        owner = 0
        for depth, bit in enumerate(order):
            if (place >> (len(order) - 1 - depth)) & 1:
                owner |= bit
        owners.append(owner)
    return np.concatenate([np.arange(per) + o * per for o in owners])


def program(potentials, orbitals, levels, occ_index, coul_rows, coul_cols):
    nv, points_dev = potentials.shape
    volume = points_dev * lax.axis_size("cell")
    orb_count = lax.axis_size("orb")
    my_rank = lax.axis_index("orb")
    per_orb = orbitals.shape[0]
    orb_bits = bits_of("orb")
    cell_bits = bits_of("cell")
    orders = [orb_bits, orb_bits[1:] + orb_bits[:1]]

    labels = jnp.arange(levels.shape[0], dtype=jnp.int32)
    marked = jnp.any(occ_index[:, None] == labels[None, :], axis=0)
    empty_all = 1.0 - marked.astype(jnp.float32)
    occ_hot = (occ_index[:, None] == labels[None, :]).astype(jnp.float32)
    occ_level = jnp.sum(occ_hot * levels[None, :], axis=1)
    basis_level = lax.dynamic_slice_in_dim(levels, my_rank * per_orb, per_orb)
    basis_empty = lax.dynamic_slice_in_dim(empty_all, my_rank * per_orb, per_orb)
    weights = -2.0 * basis_empty[None, :] / (occ_level[:, None] + basis_level[None, :])
    weights = (weights / volume).reshape(1, -1)

    owned_ids = my_rank * per_orb + jnp.arange(per_orb, dtype=jnp.int32)
    picker = (occ_index[:, None] == owned_ids[None, :]).astype(jnp.bfloat16)

    occ, inter = gather_project(picker, orbitals, potentials)
    scale = weights
    for bit in cell_bits:
        inter = halve(inter, "cell", bit, 1, None if bit == 1 else jnp.bfloat16)
        half = scale.shape[1] // 2
        scale = lax.dynamic_slice_in_dim(scale, upper("cell", bit) * half, half, 1)
    guess = (inter * scale).astype(jnp.bfloat16)
    for bit in cell_bits[::-1]:
        guess = double(guess, "cell", bit, 1)

    rows = np.concatenate([owner_order(nv, orb_count, order) for order in orders])
    place = jnp.asarray(rows[:, None] == np.arange(nv)[None, :], jnp.bfloat16)
    both = jnp.dot(place, guess, preferred_element_type=jnp.float32).astype(jnp.bfloat16)
    owned_sum = respond(both, occ, orbitals)

    row_count = points_dev // SIDE
    held = owned_sum.shape[0]
    plane = jnp.dot(
        owned_sum.reshape(held * row_count, SIDE), coul_cols.T, precision=lax.Precision.HIGHEST
    )
    stack = plane.astype(jnp.bfloat16).reshape(held, row_count, SIDE)
    offsets = [0]
    for bit in cell_bits[::-1]:
        stack = jnp.concatenate([stack, swap(stack, "cell", bit)], 1)
        offsets = offsets + [o ^ bit for o in offsets]
    my_cell = lax.axis_index("cell")
    my_rows = lax.dynamic_slice_in_dim(coul_rows, my_cell * row_count, row_count, 0)
    mixer = jnp.concatenate(
        [
            lax.dynamic_slice_in_dim(my_rows, (my_cell ^ o) * row_count, row_count, 1)
            for o in offsets
        ],
        1,
    )
    return mix_rows(mixer, stack)


def solution(mesh):
    placed = (P(None, "cell"), P("orb", "cell"), P(), P(), P(), P())
    return jax.shard_map(
        program, mesh=mesh, in_specs=placed, out_specs=P("orb", "cell", None), check_vma=False
    )
```
